256 devices in a mesh: row: 32 (over y, x, core), col: 8 (over z).
Axes of the slice: x: 4, y: 4, z: 8, core: 2. Of those that a mesh axis runs over, the one named last changes fastest.
Arguments:
- matrix: float32 [98304, 4096], P('row', 'col'), may hold values from -6 to 6
Outputs:
- top_rows: float32 [4096, 256], P(('col', 'row'))
- remainder: float32 [98304, 4096], P('row', 'col')
The draws below stay inside these ranges and needn't reach their ends.
All inputs are finite; a program needn't handle non-finite values.
Results may differ from the reference program's by a relative error of at most 0.00013.
Values sent between devices are 32-bit elements; how exact they have to be, the bound alone decides.
A program may use at most 64 MiB of HBM per device.

```python
import jax
import jax.numpy as jnp
from jax import lax

PANEL = 256
M = 98304
N = 4096


def block_scale(stream_key, dims, shards, least, top_value):
    level = 1.0
    for position, parts in shards:
        steps = jax.random.uniform(jax.random.fold_in(jax.random.fold_in(stream_key, 6), position), (parts,), jnp.float32, least / len(shards), top_value / len(shards))
        level = level * jnp.repeat(jnp.exp(steps), dims[position] // parts).reshape((-1,) + (1,) * (len(dims) - 1 - position))
    return level


def scatter_about(own_key, shape, scale, reach, shards=(), dtype=jnp.bfloat16):
    factor_of = block_scale(own_key, shape, shards, -0.22, 0.18) if shards else 1.0
    array = jax.random.normal(own_key, shape, jnp.float32) * scale * factor_of
    return jnp.minimum(jnp.maximum(array, -reach), reach).astype(dtype)


def setup_inputs(seed: int = 0) -> dict:
    key_list = jax.random.split(jax.random.key(seed), 2)
    matrix = scatter_about(key_list[0], (M, N), 1.0, 6.0, ((0, 32), (1, 8)), jnp.float32)
    return {"matrix": matrix}


def reference(matrix):
    highest = lax.Precision.HIGHEST
    panel_cols = matrix[:, :PANEL]
    gram_matrix = jnp.dot(panel_cols.T.astype(jnp.float32), panel_cols.astype(jnp.float32), precision=highest, preferred_element_type=jnp.float32)
    lower_factor = jnp.linalg.cholesky(gram_matrix)
    products = jnp.dot(matrix.T.astype(jnp.float32), panel_cols.astype(jnp.float32), precision=highest, preferred_element_type=jnp.float32)
    top_rows = lax.linalg.triangular_solve(lower_factor, products, left_side=False, lower=True, transpose_a=True)
    coeffs = lax.linalg.triangular_solve(lower_factor, top_rows, left_side=False, lower=True)
    remainder = matrix - jnp.dot(panel_cols.astype(jnp.float32), coeffs.T.astype(jnp.float32), precision=highest, preferred_element_type=jnp.float32)
    return (top_rows, remainder)
```

```python
import functools

import jax
import jax.numpy as jnp
from jax import lax
from jax.experimental import pallas as pl
from jax.experimental.pallas import tpu as pltpu
from jax.sharding import PartitionSpec as P

PANEL = 256
PIECE = 32
CHUNK = 128
LAG = CHUNK // PIECE
TILE = 128
NB = 64
MESH = pl.DeviceIdType.MESH
F32 = jnp.float32
BF16 = jnp.bfloat16


def halves(x):
    high = x.astype(BF16)
    return high, (x - high.astype(F32)).astype(BF16)


def dot_split(left, right):
    lh, ll = halves(left)
    rh, rl = halves(right)
    return jnp.dot(
        jnp.concatenate([lh, ll, lh], axis=1),
        jnp.concatenate([rh, rh, rl], axis=0),
        preferred_element_type=F32,
    )


def dot_full(left, right, contract):
    return lax.dot_general(
        left,
        right,
        ((contract[:1], contract[1:]), ((), ())),
        precision=lax.Precision.HIGHEST,
        preferred_element_type=F32,
    )


def factor_inverse(full, work, w_buf):
    row = lax.broadcasted_iota(jnp.int32, (PANEL, PANEL), 0)
    col = lax.broadcasted_iota(jnp.int32, (PANEL, PANEL), 1)
    work[:, :PANEL] = full[:PANEL, :]
    work[:, PANEL:] = jnp.where(row == col, 1.0, 0.0).astype(F32)
    r = lax.broadcasted_iota(jnp.int32, (NB, 2 * NB), 0)
    c = lax.broadcasted_iota(jnp.int32, (NB, 2 * NB), 1)
    wide = lax.broadcasted_iota(jnp.int32, (NB, PANEL), 1)
    for b in range(PANEL // NB):
        pair = b // 2 * 2 * NB
        own, other = (0, NB) if b % 2 == 0 else (NB, 0)
        tile = work[b * NB : (b + 1) * NB, pair : pair + 2 * NB]
        x = pltpu.roll(tile, NB, 1)
        mine = jnp.logical_and(c >= own, c < own + NB)
        x = jnp.where(mine, jnp.where(c - own == r, 1.0, 0.0).astype(F32), x)
        for k in range(0, NB, 2):
            k0, k1 = other + k, other + k + 1
            col0 = jnp.broadcast_to(x[:, k0 : k0 + 1], x.shape)
            col1 = jnp.broadcast_to(x[:, k1 : k1 + 1], x.shape)
            row0 = jnp.broadcast_to(x[k : k + 1, :], x.shape)
            row1 = jnp.broadcast_to(x[k + 1 : k + 2, :], x.shape)
            p00 = jnp.broadcast_to(col0[k : k + 1, :], x.shape)
            p01 = jnp.broadcast_to(col1[k : k + 1, :], x.shape)
            p11 = jnp.broadcast_to(col1[k + 1 : k + 2, :], x.shape)
            inv0 = 1.0 / p00
            ratio = p01 * inv0
            inv1 = 1.0 / (p11 - p01 * ratio)
            f0 = jnp.where(r > k, col0 * inv0, 0.0)
            row1 = row1 - ratio * row0
            f1 = jnp.where(r > k + 1, (col1 - col0 * ratio) * inv1, 0.0)
            x = x - f0 * row0 - f1 * row1
        pivot = jnp.sum(jnp.where(c - other == r, x, 0.0), axis=1, keepdims=True)
        inverse = jnp.where(mine, x, 0.0) * (1.0 / jnp.sqrt(pivot))
        rows = dot_full(inverse, work[pair : pair + 2 * NB, :], (1, 0))
        w_buf[b * NB : (b + 1) * NB, :] = rows[:, PANEL:]
        if b < PANEL // NB - 1:
            below = jnp.where(wide >= (b + 1) * NB, rows[:, :PANEL], 0.0)
            work[...] = work[...] - dot_full(below, rows, (0, 0))


def panel_kernel(
    chips, wide, planes,
    a_hbm, p_out, c_out, t_out,
    a_buf, p_buf, acc, x_buf, s_buf, rs_buf, full, t_buf, w_buf, work,
    p_recv, up_send, down_send, w_recv, w_up, w_down,
    x_send, x_recv, rs_send, rs_recv, ag_send, ag_recv, fw_send, fw_recv, local,
):
    row, z = lax.axis_index("row"), lax.axis_index("col")
    rows, cols = a_buf.shape
    block = cols // (2 * chips)
    high = chips // wide
    chip, core = lax.div(row, 2), lax.rem(row, 2)
    cy, cx = lax.div(chip, wide), lax.rem(chip, wide)
    partner = row + 1 - 2 * core
    pieces = rows // PIECE
    steps = pieces // 2 + planes // 2 * LAG
    w_pieces = PANEL // PIECE

    reach = lambda d, n: min(d, n - d)
    offsets = sorted(
        ((dy, dx) for dy in range(high) for dx in range(wide) if dy or dx),
        key=lambda o: (reach(o[0], high) + reach(o[1], wide), o),
    )

    def there(dy, dx):
        return lax.rem(cy + dy, high) * wide + lax.rem(cx + dx, wide)

    def back(dy, dx):
        return there(high - dy, wide - dx)

    from_hbm = pltpu.make_async_copy(a_hbm, a_buf, local.at[0])
    top, half = pl.ds(0, rows // 2), pl.ds(rows // 2, rows // 2)
    load_top = pltpu.make_async_copy(a_hbm.at[top, pl.ds(0, PANEL)], p_buf.at[top, :], local.at[1])
    load_half = pltpu.make_async_copy(a_hbm.at[half, pl.ds(0, PANEL)], p_buf.at[half, :], local.at[2])

    @pl.when(z == 0)
    def _():
        load_top.start()
        load_half.start()

    from_hbm.start()

    barrier = pltpu.get_barrier_semaphore()
    around = [(row, lax.rem(z + 1, planes)), (row, lax.rem(z + planes - 1, planes)), (partner, z)]
    around += [(2 * there(*o) + core, z) for o in offsets]
    for device in around:
        pl.semaphore_signal(barrier, inc=1, device_id=device, device_id_type=MESH)
    acc[...] = jnp.zeros_like(acc)
    pl.semaphore_wait(barrier, len(around))

    def hop(i, plane, sends):
        part = pl.ds(pl.multiple_of(i * PIECE, PIECE), PIECE)
        return pltpu.make_async_remote_copy(
            src_ref=p_buf.at[part, :], dst_ref=p_buf.at[part, :],
            send_sem=sends.at[i], recv_sem=p_recv.at[i],
            device_id=(row, plane), device_id_type=MESH,
        )

    def w_hop(i, plane, sends):
        part = pl.ds(i * PIECE, PIECE)
        return pltpu.make_async_remote_copy(
            src_ref=w_buf.at[part, :], dst_ref=w_buf.at[part, :],
            send_sem=sends.at[i], recv_sem=w_recv.at[i],
            device_id=(row, plane), device_id_type=MESH,
        )

    def product(start, depth):
        part = pl.ds(start, depth)
        panel = p_buf[part, :]
        for tile in range(cols // TILE):
            out = slice(tile * TILE, (tile + 1) * TILE)
            acc[out, :] += dot_split(a_buf[part, out].T, panel)

    def product_tile(chunk, tile):
        part = pl.ds(pl.multiple_of(chunk * CHUNK, CHUNK), CHUNK)
        out = pl.ds(pl.multiple_of(tile * TILE, TILE), TILE)
        acc[out, :] += dot_split(a_buf[part, out].T, p_buf[part, :])

    last = planes - 1
    received = steps - z * LAG
    up_count = jnp.where(z < last, received - LAG, 0)
    down_count = jnp.where(z == 0, steps - LAG, jnp.where(z > 1, steps - (planes - z + 1) * LAG, 0))
    above = lax.rem(z + 1, planes)
    below = jnp.where(z == 0, last, z - 1)

    @pl.when(z == 0)
    def _():
        load_top.wait()
        load_half.wait()

        @pl.loop(0, steps - LAG)
        def _(i):
            hop(i, above, up_send).start()
            hop(pieces - 1 - i, below, down_send).start()

        from_hbm.wait()

        @pl.loop(0, rows // (2 * CHUNK))
        def _(i):
            product(pl.multiple_of(i * 2 * CHUNK, 2 * CHUNK), 2 * CHUNK)

    @pl.when(z != 0)
    def _():
        from_hbm.wait()

        @pl.loop(0, steps)
        def _(t):
            i = t - z * LAG
            j = t - (planes - z) * LAG

            @pl.when(i >= 0)
            def _():
                hop(i, above, up_send).wait_recv()

                @pl.when(i < up_count)
                def _():
                    hop(i, above, up_send).start()

            @pl.when(j >= 0)
            def _():
                hop(pieces - 1 - j, below, down_send).wait_recv()

                @pl.when(j < down_count)
                def _():
                    hop(pieces - 1 - j, below, down_send).start()

            @pl.when(i >= LAG)
            def _():
                product_tile(lax.div(i, LAG) - 1, lax.rem(i, LAG))

            @pl.when(j >= LAG)
            def _():
                product_tile(rows // CHUNK - lax.div(j, LAG), lax.rem(j, LAG))

        product(pl.multiple_of(received * PIECE - CHUNK, CHUNK), 2 * CHUNK)

    save_panel = pltpu.make_async_copy(p_buf, p_out, local.at[3])
    save_panel.start()

    def at(q, c):
        return pl.ds(pl.multiple_of((2 * q + c) * block, 8), block)

    def slot(q):
        return pl.ds(pl.multiple_of(q * block, 8), block)

    def swap(q):
        return pltpu.make_async_remote_copy(
            src_ref=acc.at[at(q, 1 - core), :], dst_ref=x_buf.at[slot(q), :],
            send_sem=x_send.at[q], recv_sem=x_recv.at[q],
            device_id=(partner, z), device_id_type=MESH,
        )

    def scatter(q, source):
        return pltpu.make_async_remote_copy(
            src_ref=s_buf.at[slot(q), :], dst_ref=rs_buf.at[slot(source), :],
            send_sem=rs_send.at[q], recv_sem=rs_recv.at[source],
            device_id=(2 * q + core, z), device_id_type=MESH,
        )

    order = offsets[::-1]
    for o in order + [(0, 0)]:
        swap(there(*o)).start()
    for o in order:
        q = there(*o)
        swap(q).wait_recv()
        s_buf[slot(q), :] = acc[at(q, core), :] + x_buf[slot(q), :]
        scatter(q, chip).start()
    swap(chip).wait_recv()
    total = acc[at(chip, core), :] + x_buf[slot(chip), :]

    @pl.when(z != 0)
    def _():
        up = z <= planes // 2
        for i in range(w_pieces):
            w_hop(i, above, w_up).wait_recv()

            @pl.when(z < planes // 2)
            def _():
                w_hop(i, above, w_up).start()

            @pl.when(z > planes // 2 + 1)
            def _():
                w_hop(i, below, w_down).start()

    for o in offsets:
        q = back(*o)
        scatter(q, q).wait_recv()
        total = total + rs_buf[slot(q), :]

    mine = at(chip, core)

    @pl.when(z == 0)
    def _():
        full[mine, :] = total

    @pl.when(z != 0)
    def _():
        top = dot_full(total, w_buf[...], (1, 1))
        t_buf[...] = top
        full[mine, :] = dot_full(top, w_buf[...], (1, 0))

    def gather(q, source):
        return pltpu.make_async_remote_copy(
            src_ref=full.at[mine, :], dst_ref=full.at[at(source, core), :],
            send_sem=ag_send.at[q], recv_sem=ag_recv.at[source],
            device_id=(2 * q + core, z), device_id_type=MESH,
        )

    def pass_on(q, c):
        return pltpu.make_async_remote_copy(
            src_ref=full.at[at(q, c), :], dst_ref=full.at[at(q, c), :],
            send_sem=fw_send.at[q], recv_sem=fw_recv.at[q],
            device_id=(partner, z), device_id_type=MESH,
        )

    for o in order:
        gather(there(*o), chip).start()
    pass_on(chip, core).start()
    for o in offsets:
        q = back(*o)
        gather(q, q).wait_recv()
        pass_on(q, core).start()
    for o in [(0, 0)] + offsets:
        pass_on(back(*o), 1 - core).wait_recv()

    for o in offsets:
        gather(there(*o), chip).wait_send()
    for o in [(0, 0)] + offsets:
        pass_on(there(*o), core).wait_send()

    @pl.when(z == 0)
    def _():
        factor_inverse(full, work, w_buf)
        for i in range(w_pieces):
            w_hop(i, above, w_up).start()
            w_hop(i, below, w_down).start()
        t_buf[...] = dot_full(full[mine, :], w_buf[...], (1, 1))
        tops = dot_full(full[...], w_buf[...], (1, 1))
        full[...] = dot_full(tops, w_buf[...], (1, 0))

    save_coeffs = pltpu.make_async_copy(full, c_out, local.at[4])
    save_top = pltpu.make_async_copy(t_buf, t_out, local.at[5])
    save_coeffs.start()
    save_top.start()

    for o in offsets:
        scatter(there(*o), chip).wait_send()
    for o in [(0, 0)] + offsets:
        swap(there(*o)).wait_send()

    @pl.loop(0, up_count)
    def _(i):
        hop(i, above, up_send).wait_send()

    @pl.loop(0, down_count)
    def _(i):
        hop(pieces - 1 - i, below, down_send).wait_send()

    @pl.when(z < planes // 2)
    def _():
        for i in range(w_pieces):
            w_hop(i, above, w_up).wait_send()

    @pl.when(jnp.logical_or(z == 0, z > planes // 2 + 1))
    def _():
        for i in range(w_pieces):
            w_hop(i, below, w_down).wait_send()

    save_panel.wait()
    save_coeffs.wait()
    save_top.wait()


def panel_step(matrix, chips, planes):
    rows, cols = matrix.shape
    block = cols // (2 * chips)
    pieces = rows // PIECE
    dma = lambda n: pltpu.SemaphoreType.DMA((n,))
    anywhere = pl.BlockSpec(memory_space=pl.ANY)
    return pl.pallas_call(
        functools.partial(panel_kernel, chips, min(4, chips), planes),
        out_shape=(
            jax.ShapeDtypeStruct((rows, PANEL), F32),
            jax.ShapeDtypeStruct((cols, PANEL), F32),
            jax.ShapeDtypeStruct((block, PANEL), F32),
        ),
        in_specs=[anywhere],
        out_specs=(anywhere, anywhere, anywhere),
        scratch_shapes=[
            pltpu.VMEM((rows, cols), F32),
            pltpu.VMEM((rows, PANEL), F32),
            pltpu.VMEM((cols, PANEL), F32),
            pltpu.VMEM((cols // 2, PANEL), F32),
            pltpu.VMEM((cols // 2, PANEL), F32),
            pltpu.VMEM((cols // 2, PANEL), F32),
            pltpu.VMEM((cols, PANEL), F32),
            pltpu.VMEM((block, PANEL), F32),
            pltpu.VMEM((PANEL, PANEL), F32),
            pltpu.VMEM((PANEL, 2 * PANEL), F32),
            dma(pieces), dma(pieces), dma(pieces),
            dma(PANEL // PIECE), dma(PANEL // PIECE), dma(PANEL // PIECE),
            dma(chips), dma(chips), dma(chips), dma(chips),
            dma(chips), dma(chips), dma(chips), dma(chips),
            dma(6),
        ],
        compiler_params=pltpu.CompilerParams(
            collective_id=0, has_side_effects=True, vmem_limit_bytes=40 << 20
        ),
        name="panel_step",
    )(matrix)


def remainder_kernel(a_ref, p_ref, c_ref, o_ref, c_split):
    @pl.when(pl.program_id(0) == 0)
    def _():
        high, low = halves(c_ref[...])
        c_split[:, :PANEL] = high
        c_split[:, PANEL : 2 * PANEL] = high
        c_split[:, 2 * PANEL :] = low

    high, low = halves(p_ref[...])
    o_ref[...] = a_ref[...] - lax.dot_general(
        jnp.concatenate([high, low, high], axis=1),
        c_split[...],
        (((1,), (1,)), ((), ())),
        preferred_element_type=F32,
    )


def remainder_step(matrix, panel, coeffs, tile=512):
    rows, cols = matrix.shape
    return pl.pallas_call(
        remainder_kernel,
        out_shape=jax.ShapeDtypeStruct((rows, cols), F32),
        grid=(rows // tile,),
        in_specs=[
            pl.BlockSpec((tile, cols), lambda i: (i, 0)),
            pl.BlockSpec((tile, PANEL), lambda i: (i, 0)),
            pl.BlockSpec((cols, PANEL), lambda i: (0, 0)),
        ],
        out_specs=pl.BlockSpec((tile, cols), lambda i: (i, 0)),
        scratch_shapes=[pltpu.VMEM((cols, 3 * PANEL), BF16)],
        compiler_params=pltpu.CompilerParams(vmem_limit_bytes=24 << 20),
        name="remainder_step",
    )(matrix, panel, coeffs)


def solution(mesh):
    chips, planes = mesh.shape["row"] // 2, mesh.shape["col"]

    def shards(matrix):
        panel, coeffs, top_rows = panel_step(matrix, chips, planes)
        return top_rows, remainder_step(matrix, panel, coeffs)

    return jax.shard_map(
        shards,
        mesh=mesh,
        in_specs=(P("row", "col"),),
        out_specs=(P(("col", "row"), None), P("row", "col")),
        check_vma=False,
    )
```
